32 devices in a mesh: dp: 8 (over y, x, core), ctx: 4 (over z).
Axes of the slice: x: 2, y: 2, z: 4, core: 2. Of those that a mesh axis runs over, the one named last changes fastest.
Arguments:
- queries: bfloat16 [16384, 512], P(('dp', 'ctx')), parts along dimension 0, may hold values from -60 to 60
- key_vectors: bfloat16 [16384, 128], P(('dp', 'ctx')), parts along dimension 0, may hold values from -20 to 20
- value_vectors: bfloat16 [16384, 128], P(('dp', 'ctx')), parts along dimension 0, may hold values from -6 to 6
- block_plan: int32 [64], P('dp'), parts along dimension 0, may hold values from 0 to 7, each once
- doc_lengths: int32 [64], P('dp'), parts along dimension 0, may hold values from 1 to 1024, 2048 in all
- out_weight: bfloat16 [512, 4096], P(None, 'ctx'), may hold values from -0.25 to 0.25
Outputs:
- output: bfloat16 [16384, 4096], P(('dp', 'ctx')), parts along dimension 0
The draws below stay inside these ranges and needn't reach their ends.
There are 8 independent parts, one for each index of `dp`. The reference program is written for one: setup_inputs(seed, part) draws one part's arguments, and reference() takes and returns one part's arrays. A program takes and returns all parts, laid end to end along the dimension named above; an argument that names none is the same for every part. Nothing has to cross between parts.
Inputs may be any that keep to these rules, and one draw needn't show every extreme that they name: `doc_lengths`: the 8 lengths sum to 2048.
All inputs are finite; a program needn't handle non-finite values.
Results may differ from the reference program's by a relative error of at most 0.013.
Values may be sent and summed in bfloat16 or wider, within the bound.
No kernel may reach another device: no remote copies, remote signals or barrier semaphores. Data moves between devices by JAX's collectives and lax.ppermute only.
A program may use at most 64 MiB of HBM per device.

```python
import math
import jax
import jax.numpy as jnp
import numpy as np
from jax import lax

D = 4096
HD = 128
G = 4
SPAN = 512
NDOCS = 8
HALF = 256
LENGTH = 2048
NBLOCKS = 8
N_CTX = 4


def shared_base(key):
    return jnp.clip(jax.random.normal(jax.random.fold_in(key, 11), (LENGTH, HD), jnp.float32), -4.5, 4.5)


def draw_key_vectors(key, part):
    base = shared_base(key)
    result = base
    return result.astype(jnp.bfloat16)


def draw_queries(key, part):
    result = jnp.clip(jax.random.normal(jax.random.fold_in(key, 3), (LENGTH, G * HD), jnp.float32), -6.0, 6.0)
    return result.astype(jnp.bfloat16)


def level_of(own_key, dims, pieces, low, largest):
    def one(position, blocks):
        steps = jax.random.uniform(jax.random.fold_in(jax.random.fold_in(own_key, 6), position), (blocks,), jnp.float32, low / len(pieces), largest / len(pieces))
        return jnp.repeat(jnp.exp(steps), dims[position] // blocks).reshape((-1,) + (1,) * (len(dims) - position - 1))

    loudness = one(*pieces[0])
    for cut in pieces[1:]:
        loudness = loudness * one(*cut)
    return loudness


def profile(count, total, bound, slope):
    portions = [(1 << 20) // math.isqrt(standing ** slope) + 1 for standing in range(2, count + 1)]
    rest, counts = total - bound - (count - 1), [1] * (count - 1)
    while rest > 0:
        movable = [i for i in range(count - 1) if counts[i] < bound]
        pool, budget = sum([portions[i] for i in movable]), rest
        for i in movable:
            more = min(bound - counts[i], max(1, budget * portions[i] // pool), rest)
            counts[i] = counts[i] + more
            rest = rest - more
    return np.array([bound] + counts)


def uneven(key, count, total, bound, skew):
    if count == 2:
        one = jax.random.randint(key, (), max(1, total - bound), min(bound, total - 1) + 1)
        return jnp.stack([one, total - one])
    lengths = jnp.asarray(profile(count, total, bound, skew), jnp.int32)
    twos = (count - 1) // 2
    donor, sink = lengths[1:1 + 2 * twos:2], lengths[2:2 + 2 * twos:2]
    slack = jnp.minimum(donor - 1, bound - sink)
    passed = jax.random.randint(jax.random.fold_in(key, 1), (twos,), 0, 1 << 20) % (slack + 1)
    lengths = lengths.at[1:1 + 2 * twos:2].set(donor - passed).at[2:2 + 2 * twos:2].set(sink + passed)
    return lengths[jax.random.permutation(jax.random.fold_in(key, 2), count)]


def noise(rng, extent, deviation, most, cuts=(), kind=jnp.bfloat16):
    values = deviation * jax.random.normal(rng, extent, jnp.float32)
    if cuts:
        values = values * level_of(rng, extent, cuts, -0.22, 0.18)
    return jnp.clip(values, -most, most).astype(kind)


def setup_inputs(seed: int = 0, part: int = 0) -> dict:
    keys = jax.random.split(jax.random.key(seed), 7)
    own_keys = jax.random.split(jax.random.fold_in(keys[6], part), 7)
    queries = draw_queries(jax.random.fold_in(jax.random.fold_in(keys[6], part), 71), part)
    key_vectors = draw_key_vectors(jax.random.fold_in(jax.random.fold_in(keys[6], part), 71), part)
    value_vectors = noise(own_keys[2], (LENGTH, HD), 1.0, 6.0, ((0, 4),))
    block_plan = jax.random.permutation(own_keys[3], NBLOCKS).astype(jnp.int32)
    doc_lengths = uneven(own_keys[4], NDOCS, LENGTH, LENGTH // 2, 2).astype(jnp.int32)
    out_weight = noise(keys[5], (G * HD, D), (G * HD) ** -0.5, 0.25, ((1, 4),))
    return dict(queries=queries, key_vectors=key_vectors, value_vectors=value_vectors, block_plan=block_plan, doc_lengths=doc_lengths, out_weight=out_weight)


def reference(queries, key_vectors, value_vectors, block_plan, doc_lengths, out_weight):
    row_ids = jnp.arange(LENGTH, dtype=jnp.int32)
    positions = (block_plan[row_ids // HALF] * HALF + row_ids % HALF).astype(jnp.int32)
    doc_ends = jnp.cumsum(doc_lengths).astype(jnp.int32)
    documents = lax.optimization_barrier(jnp.sum((positions[:, None] >= doc_ends[None, :]).astype(jnp.int32), axis=1))
    keys_wide = key_vectors.astype(jnp.float32)
    values_wide = value_vectors.astype(jnp.float32)
    score_scale = 1.0 / math.sqrt(HD)

    def attend(block_index):
        first_row = (block_index * SPAN).astype(jnp.int32)
        query_block = lax.dynamic_slice_in_dim(queries, first_row, SPAN, 0).astype(jnp.float32).reshape(SPAN, G, HD)
        query_pos = lax.dynamic_slice_in_dim(positions, first_row, SPAN, 0)
        query_doc = lax.dynamic_slice_in_dim(documents, first_row, SPAN, 0)
        allowed = (positions[None, :] <= query_pos[:, None]) & (documents[None, :] == query_doc[:, None])
        scores = jnp.einsum('rgd,kd->grk', query_block, keys_wide) * score_scale
        scores = jnp.where(allowed[None], scores, jnp.float32(-1e+30))
        row_max = lax.optimization_barrier(jnp.max(scores, axis=2, keepdims=True))
        weights = jnp.where(allowed[None], jnp.exp(scores - row_max), jnp.float32(0.0))
        row_total = lax.optimization_barrier(jnp.sum(weights, axis=2))
        probs = lax.optimization_barrier(weights.astype(jnp.bfloat16)).astype(jnp.float32)
        weighted = jnp.einsum('grk,kd->rgd', probs, values_wide)
        attended = weighted / jnp.transpose(row_total)[:, :, None]
        return attended.reshape(SPAN, G * HD).astype(jnp.bfloat16)
    blocks = lax.map(attend, jnp.arange(N_CTX, dtype=jnp.int32))
    attended = blocks.reshape(LENGTH, G * HD)
    return jnp.dot(attended, out_weight, preferred_element_type=jnp.float32).astype(jnp.bfloat16)
```

```python
import functools
import math

import jax
import jax.numpy as jnp
from jax import lax
from jax.experimental import pallas as pl
from jax.experimental.pallas import tpu as pltpu
from jax.sharding import PartitionSpec as P


NEG = -1e30
MIB = 1 << 20


def order_of(ctx):
    return sorted(range(1, ctx), key=lambda s: (min(s, ctx - s), s))


def doc_start(lengths_ref, position):
    end = jnp.int32(0)
    start = jnp.zeros_like(position)
    for i in range(lengths_ref.shape[0]):
        end = end + lengths_ref[i]
        start = jnp.maximum(start, jnp.where(position >= end, end, 0))
    return start


def scalar_start(lengths_ref, position):
    end = jnp.int32(0)
    start = jnp.int32(0)
    for i in range(lengths_ref.shape[0]):
        end = end + lengths_ref[i]
        start = jnp.maximum(start, jnp.where(position >= end, end, 0))
    return start


def attend_pair(dims, first, diagonal, q_blk, k_blk, start, key_base, q_ref, kv_ref, m_ref, l_ref, acc_ref):
    half, hd, heads, scale = dims
    key = kv_ref[k_blk * half:(k_blk + 1) * half, :hd]
    value_t = kv_ref[k_blk * half:(k_blk + 1) * half, hd:].astype(jnp.float32).T.astype(jnp.bfloat16)
    key_ids = lax.broadcasted_iota(jnp.int32, (half, half), 0)
    keep = key_ids >= start - key_base
    if diagonal:
        keep = keep & (key_ids <= lax.broadcasted_iota(jnp.int32, (half, half), 1))
    bias = jnp.where(keep, jnp.float32(0.0), jnp.float32(NEG))
    for h in range(heads):
        row = q_blk * heads + h
        query = q_ref[q_blk * half:(q_blk + 1) * half, h * hd:(h + 1) * hd]
        s = lax.dot_general(key, query, (((1,), (1,)), ((), ())), preferred_element_type=jnp.float32)
        t = s * scale + bias
        top = jnp.max(t, axis=0, keepdims=True)
        if first:
            m_new = top
        else:
            m_old = m_ref[row:row + 1, :]
            m_new = jnp.maximum(m_old, top)
        p = jnp.exp2(t - m_new)
        total = jnp.sum(p, axis=0, keepdims=True)
        part = jnp.dot(value_t, p.astype(jnp.bfloat16), preferred_element_type=jnp.float32)
        if first:
            l_ref[row:row + 1, :] = total
            acc_ref[row * hd:(row + 1) * hd, :] = part
        else:
            alpha = jnp.exp2(m_old - m_new)
            l_ref[row:row + 1, :] = l_ref[row:row + 1, :] * alpha + total
            acc_ref[row * hd:(row + 1) * hd, :] = acc_ref[row * hd:(row + 1) * hd, :] * alpha + part
        m_ref[row:row + 1, :] = m_new


def attend_chunk(dims, own, me, src, plan_ref, lengths_ref, q_ref, kv_ref, m_ref, l_ref, acc_ref):
    half = dims[0]
    order = [(0, 0), (1, 1), (0, 1), (1, 0)]
    lanes = lax.broadcasted_iota(jnp.int32, (1, half), 1)
    for q_blk, k_blk in order:
        q_base = plan_ref[me * 2 + q_blk] * half
        k_base = plan_ref[src * 2 + k_blk] * half
        args = (q_ref, kv_ref, m_ref, l_ref, acc_ref)
        if own and q_blk == k_blk:
            start = doc_start(lengths_ref, q_base + lanes)
            attend_pair(dims, True, True, q_blk, k_blk, start, k_base, *args)
        else:
            need = (k_base < q_base) & (scalar_start(lengths_ref, q_base) < k_base + half)

            @pl.when(need)
            def _(q_blk=q_blk, k_blk=k_blk, q_base=q_base, k_base=k_base):
                start = doc_start(lengths_ref, q_base + lanes)
                attend_pair(dims, False, False, q_blk, k_blk, start, k_base, *args)


def own_kernel(dims, plan_ref, lengths_ref, q_ref, kv_ref, m_ref, l_ref, acc_ref):
    me = lax.axis_index("ctx")
    attend_chunk(dims, True, me, me, plan_ref, lengths_ref, q_ref, kv_ref, m_ref, l_ref, acc_ref)


def chunk_kernel(dims, ctx, shift, plan_ref, lengths_ref, q_ref, kv_ref, m_in, l_in, acc_in, m_ref, l_ref, acc_ref):
    me = lax.axis_index("ctx")
    src = lax.rem(me + shift, ctx)
    m_ref[...] = m_in[...]
    l_ref[...] = l_in[...]
    acc_ref[...] = acc_in[...]
    attend_chunk(dims, False, me, src, plan_ref, lengths_ref, q_ref, kv_ref, m_ref, l_ref, acc_ref)


def final_kernel(dims, ctx, shift, masks, groups, tile, *refs):
    half, hd, heads, _ = dims
    plan_ref, lengths_ref, q_ref, kv_ref, m_in, l_in, acc_in, w_ref = refs[:8]
    n_groups = len(groups)
    piece_refs = refs[8:8 + 2 * n_groups]
    out_ref, w_buf, att, stage, m_ref, l_ref, acc_ref, w_sem, o_sem = refs[8 + 2 * n_groups:]
    me = lax.axis_index("ctx")
    dp = lax.axis_index("dp")
    piece_rows = piece_refs[0].shape[2]
    cols = w_ref.shape[1]
    loads = {0: [pltpu.make_async_copy(w_ref, w_buf.at[0], w_sem.at[0])]}
    for g, shifts in enumerate(groups):
        for i, s in enumerate(shifts):
            loads[s] = []
            for j, mask in enumerate(masks):
                for core in range(2):
                    row = pl.multiple_of((dp ^ (mask ^ core)) * piece_rows, piece_rows)
                    loads[s].append(
                        pltpu.make_async_copy(
                            piece_refs[2 * g + core].at[j, i],
                            w_buf.at[s, pl.ds(row, piece_rows), :],
                            w_sem.at[s],
                        )
                    )
    slots = list(range(ctx))
    for s in slots:
        for load in loads[s]:
            load.start()
    m_ref[...] = m_in[...]
    l_ref[...] = l_in[...]
    acc_ref[...] = acc_in[...]
    src = lax.rem(me + shift, ctx)
    attend_chunk(dims, False, me, src, plan_ref, lengths_ref, q_ref, kv_ref, m_ref, l_ref, acc_ref)
    for q_blk in range(2):
        for h in range(heads):
            row = q_blk * heads + h
            o = acc_ref[row * hd:(row + 1) * hd, :] / l_ref[row:row + 1, :]
            att[q_blk * half:(q_blk + 1) * half, h * hd:(h + 1) * hd] = o.T.astype(jnp.bfloat16)
    stores = []
    for s in slots:
        for load in loads[s]:
            load.wait()
        base = lax.rem(me + s, ctx) * cols
        for t in range(0, cols, tile):
            y = jnp.dot(att[...], w_buf[s, :, t:t + tile], preferred_element_type=jnp.float32)
            stage[s, :, t:t + tile] = y.astype(jnp.bfloat16)
            store = pltpu.make_async_copy(
                stage.at[s, :, pl.ds(t, tile)],
                out_ref.at[:, pl.ds(pl.multiple_of(base + t, tile), tile)],
                o_sem.at[s, t // tile],
            )
            store.start()
            stores.append(store)
    for store in stores:
        store.wait()


def shards(dp_size, ctx, *args):
    return run(dp_size, ctx, *args)


def run(dp_size, ctx, queries, key_vectors, value_vectors, block_plan, doc_lengths, out_weight):
    rows, width = queries.shape
    hd = key_vectors.shape[1]
    heads = width // hd
    half = rows // 2
    cols = out_weight.shape[1]
    depth = out_weight.shape[0]
    out_cols = cols * ctx
    piece_rows = depth // dp_size
    dims = (half, hd, heads, math.log2(math.e) / math.sqrt(hd))
    near_first = order_of(ctx)
    masks = [b for b in range(0, dp_size, 2)]
    groups = [[s] for s in near_first] if ctx <= 4 else [near_first]

    def from_ctx(x, s):
        return lax.ppermute(x, "ctx", [((i + s) % ctx, i) for i in range(ctx)])

    def from_dp(x, mask):
        return lax.ppermute(x, "dp", [(i ^ mask, i) for i in range(dp_size)])

    piece = lax.dynamic_slice_in_dim(out_weight, lax.axis_index("dp") * piece_rows, piece_rows, 0)
    kv_own = jnp.concatenate([key_vectors, value_vectors], axis=1)
    w_z = {}
    for s in near_first:
        w_z[s] = from_ctx(piece, s)
    kv = {}
    for s in near_first:
        kv[s] = from_ctx(kv_own, s)

    smem = pl.BlockSpec(memory_space=pltpu.SMEM)
    vmem = pl.BlockSpec(memory_space=pltpu.VMEM)
    anyspace = pl.BlockSpec(memory_space=pl.ANY)
    state_shapes = (
        jax.ShapeDtypeStruct((2 * heads, half), jnp.float32),
        jax.ShapeDtypeStruct((2 * heads, half), jnp.float32),
        jax.ShapeDtypeStruct((2 * heads * hd, half), jnp.float32),
    )
    chunk_cost = pl.CostEstimate(
        flops=4 * heads * rows * rows * hd, bytes_accessed=3 * MIB, transcendentals=heads * rows * rows
    )
    state = pl.pallas_call(
        functools.partial(own_kernel, dims),
        out_shape=state_shapes,
        in_specs=[smem, smem, vmem, vmem],
        out_specs=(vmem,) * 3,
        compiler_params=pltpu.CompilerParams(vmem_limit_bytes=16 * MIB),
        cost_estimate=chunk_cost,
        name="attend_own",
    )(block_plan, doc_lengths, queries, kv_own)
    for s in near_first[:-1]:
        state = pl.pallas_call(
            functools.partial(chunk_kernel, dims, ctx, s),
            out_shape=state_shapes,
            in_specs=[smem, smem] + [vmem] * 5,
            out_specs=(vmem,) * 3,
            compiler_params=pltpu.CompilerParams(vmem_limit_bytes=16 * MIB),
            cost_estimate=chunk_cost,
        )(block_plan, doc_lengths, queries, kv[s], *state)

    pieces = []
    for shifts in groups:
        mine = jnp.stack([w_z[s] for s in shifts]) if len(shifts) > 1 else w_z[shifts[0]][None]
        parts = [mine]
        for mask in masks[1:]:
            parts.append(from_dp(mine, mask))
        own = jnp.stack(parts)
        other = from_dp(own, 1)
        pieces += [own, other]

    tile = min(cols, 512)
    last = near_first[-1]
    return pl.pallas_call(
        functools.partial(final_kernel, dims, ctx, last, masks, groups, tile),
        out_shape=jax.ShapeDtypeStruct((rows, out_cols), jnp.bfloat16),
        in_specs=[smem, smem] + [vmem] * 5 + [anyspace] * (1 + len(pieces)),
        out_specs=anyspace,
        scratch_shapes=[
            pltpu.VMEM((ctx, depth, cols), jnp.bfloat16),
            pltpu.VMEM((rows, width), jnp.bfloat16),
            pltpu.VMEM((ctx, rows, cols), jnp.bfloat16),
            pltpu.VMEM((2 * heads, half), jnp.float32),
            pltpu.VMEM((2 * heads, half), jnp.float32),
            pltpu.VMEM((2 * heads * hd, half), jnp.float32),
            pltpu.SemaphoreType.DMA((ctx,)),
            pltpu.SemaphoreType.DMA((ctx, cols // tile)),
        ],
        compiler_params=pltpu.CompilerParams(vmem_limit_bytes=28 * MIB),
        cost_estimate=pl.CostEstimate(
            flops=2 * rows * depth * out_cols, bytes_accessed=8 * MIB, transcendentals=0
        ),
        name="project",
    )(block_plan, doc_lengths, queries, kv[last], *state, out_weight, *pieces)


def solution(mesh):
    placed = (
        P(("dp", "ctx"), None),
        P(("dp", "ctx"), None),
        P(("dp", "ctx"), None),
        P("dp"),
        P("dp"),
        P(None, "ctx"),
    )
    body = functools.partial(shards, mesh.shape["dp"], mesh.shape["ctx"])
    return jax.shard_map(body, mesh=mesh, in_specs=placed, out_specs=P(("dp", "ctx"), None), check_vma=False)
```

```python
import functools
import math

import jax
import jax.numpy as jnp
from jax import lax
from jax.experimental import pallas as pl
from jax.experimental.pallas import tpu as pltpu
from jax.sharding import PartitionSpec as P


NEG = -1e30
MIB = 1 << 20


def doc_start(lengths_ref, position):
    end = jnp.int32(0)
    start = jnp.zeros_like(position)
    for i in range(lengths_ref.shape[0]):
        end = end + lengths_ref[i]
        start = jnp.maximum(start, jnp.where(position >= end, end, 0))
    return start


def scalar_start(lengths_ref, position):
    end = jnp.int32(0)
    start = jnp.int32(0)
    for i in range(lengths_ref.shape[0]):
        end = end + lengths_ref[i]
        start = jnp.maximum(start, jnp.where(position >= end, end, 0))
    return start


def attend_pair(dims, first, diagonal, q_blk, k_blk, start, key_base, q_ref, k_ref, v_ref, m_ref, l_ref, acc_ref):
    half, hd, heads, scale = dims
    key = k_ref[k_blk * half:(k_blk + 1) * half, :]
    value_t = v_ref[k_blk * half:(k_blk + 1) * half, :].astype(jnp.float32).T.astype(jnp.bfloat16)
    key_ids = lax.broadcasted_iota(jnp.int32, (half, half), 0)
    keep = key_ids >= start - key_base
    if diagonal:
        keep = keep & (key_ids <= lax.broadcasted_iota(jnp.int32, (half, half), 1))
    bias = jnp.where(keep, jnp.float32(0.0), jnp.float32(NEG))
    for h in range(heads):
        row = q_blk * heads + h
        query = q_ref[q_blk * half:(q_blk + 1) * half, h * hd:(h + 1) * hd]
        s = lax.dot_general(key, query, (((1,), (1,)), ((), ())), preferred_element_type=jnp.float32)
        t = s * scale + bias
        top = jnp.max(t, axis=0, keepdims=True)
        if first:
            m_new = top
        else:
            m_old = m_ref[row:row + 1, :]
            m_new = jnp.maximum(m_old, top)
        p = jnp.exp2(t - m_new)
        total = jnp.sum(p, axis=0, keepdims=True)
        part = jnp.dot(value_t, p.astype(jnp.bfloat16), preferred_element_type=jnp.float32)
        if first:
            l_ref[row:row + 1, :] = total
            acc_ref[row * hd:(row + 1) * hd, :] = part
        else:
            alpha = jnp.exp2(m_old - m_new)
            l_ref[row:row + 1, :] = l_ref[row:row + 1, :] * alpha + total
            acc_ref[row * hd:(row + 1) * hd, :] = acc_ref[row * hd:(row + 1) * hd, :] * alpha + part
        m_ref[row:row + 1, :] = m_new


def attend_chunk(dims, own, me, src, plan_ref, lengths_ref, *args):
    half = dims[0]
    order = [(0, 0), (1, 1), (0, 1), (1, 0)]
    lanes = lax.broadcasted_iota(jnp.int32, (1, half), 1)
    for q_blk, k_blk in order:
        q_base = plan_ref[me * 2 + q_blk] * half
        k_base = plan_ref[src * 2 + k_blk] * half
        if own and q_blk == k_blk:
            start = doc_start(lengths_ref, q_base + lanes)
            attend_pair(dims, True, True, q_blk, k_blk, start, k_base, *args)
        else:
            need = (k_base < q_base) & (scalar_start(lengths_ref, q_base) < k_base + half)

            @pl.when(need)
            def _(q_blk=q_blk, k_blk=k_blk, q_base=q_base, k_base=k_base):
                start = doc_start(lengths_ref, q_base + lanes)
                attend_pair(dims, False, False, q_blk, k_blk, start, k_base, *args)


def own_kernel(dims, plan_ref, lengths_ref, q_ref, k_ref, v_ref, m_ref, l_ref, acc_ref):
    me = lax.axis_index("ctx")
    attend_chunk(dims, True, me, me, plan_ref, lengths_ref, q_ref, k_ref, v_ref, m_ref, l_ref, acc_ref)


def copy_state(sources, targets):
    for source, target in zip(sources, targets):
        target[...] = source[...]


def chunk_kernel(dims, shift, plan_ref, lengths_ref, q_ref, k_ref, v_ref, m_in, l_in, acc_in, m_ref, l_ref, acc_ref):
    me = lax.axis_index("ctx")
    copy_state((m_in, l_in, acc_in), (m_ref, l_ref, acc_ref))
    attend_chunk(dims, False, me, me ^ shift, plan_ref, lengths_ref, q_ref, k_ref, v_ref, m_ref, l_ref, acc_ref)


def assemble_kernel(masks, *refs):
    part_refs, full_ref = refs[:-1], refs[-1]
    dp = lax.axis_index("dp")
    rows = part_refs[0].shape[1]
    for j, mask in enumerate(masks):
        for core in range(2):
            row = pl.multiple_of((dp ^ (mask ^ core)) * rows, rows)
            for i in range(full_ref.shape[0]):
                full_ref[i, pl.ds(row, rows), :] = part_refs[2 * j + core][i]


def final_kernel(dims, shift, groups, tile, *refs):
    half, hd, heads, _ = dims
    plan_ref, lengths_ref, q_ref, k_ref, v_ref, m_in, l_in, acc_in, w_ref = refs[:9]
    full_refs = refs[9:9 + len(groups)]
    out_ref, att, stage, m_ref, l_ref, acc_ref, o_sem = refs[9 + len(groups):]
    me = lax.axis_index("ctx")
    cols = w_ref.shape[1]
    copy_state((m_in, l_in, acc_in), (m_ref, l_ref, acc_ref))
    attend_chunk(dims, False, me, me ^ shift, plan_ref, lengths_ref, q_ref, k_ref, v_ref, m_ref, l_ref, acc_ref)
    for q_blk in range(2):
        for h in range(heads):
            row = q_blk * heads + h
            o = acc_ref[row * hd:(row + 1) * hd, :] / l_ref[row:row + 1, :]
            att[q_blk * half:(q_blk + 1) * half, h * hd:(h + 1) * hd] = o.T.astype(jnp.bfloat16)
    weights = [(0, w_ref)]
    for full_ref, shifts in zip(full_refs, groups):
        weights += [(s, full_ref.at[i]) for i, s in enumerate(shifts)]
    stores = []
    for slot, (s, weight) in enumerate(weights):
        base = (me ^ s) * cols
        for t in range(0, cols, tile):
            y = jnp.dot(att[...], weight[:, t:t + tile], preferred_element_type=jnp.float32)
            stage[slot, :, t:t + tile] = y.astype(jnp.bfloat16)
            store = pltpu.make_async_copy(
                stage.at[slot, :, pl.ds(t, tile)],
                out_ref.at[:, pl.ds(pl.multiple_of(base + t, tile), tile)],
                o_sem.at[slot, t // tile],
            )
            store.start()
            stores.append(store)
    for store in stores:
        store.wait()


def shards(dp_size, ctx, *args):
    return run(dp_size, ctx, *args)


def run(dp_size, ctx, queries, key_vectors, value_vectors, block_plan, doc_lengths, out_weight):
    rows, width = queries.shape
    hd = key_vectors.shape[1]
    heads = width // hd
    half = rows // 2
    depth, cols = out_weight.shape
    out_cols = cols * ctx
    piece_rows = depth // dp_size
    dims = (half, hd, heads, math.log2(math.e) / math.sqrt(hd))
    shifts = list(range(1, ctx))
    masks = list(range(0, dp_size, 2))
    groups = groups_of(ctx)

    def from_ctx(x, s):
        return lax.ppermute(x, "ctx", [(i ^ s, i) for i in range(ctx)])

    def from_dp(x, mask):
        return lax.ppermute(x, "dp", [(i ^ mask, i) for i in range(dp_size)])

    keys, values, w_z = {}, {}, {}
    for s in shifts:
        keys[s] = from_ctx(key_vectors, s)
        values[s] = from_ctx(value_vectors, s)
    piece = lax.dynamic_slice_in_dim(out_weight, lax.axis_index("dp") * piece_rows, piece_rows, 0)
    for s in shifts:
        w_z[s] = from_ctx(piece, s)

    smem = pl.BlockSpec(memory_space=pltpu.SMEM)
    vmem = pl.BlockSpec(memory_space=pltpu.VMEM)
    anyspace = pl.BlockSpec(memory_space=pl.ANY)
    state_shapes = (
        jax.ShapeDtypeStruct((2 * heads, half), jnp.float32),
        jax.ShapeDtypeStruct((2 * heads, half), jnp.float32),
        jax.ShapeDtypeStruct((2 * heads * hd, half), jnp.float32),
    )
    chunk_cost = pl.CostEstimate(
        flops=4 * heads * rows * rows * hd, bytes_accessed=3 * MIB, transcendentals=heads * rows * rows
    )
    state = pl.pallas_call(
        functools.partial(own_kernel, dims),
        out_shape=state_shapes,
        in_specs=[smem, smem, vmem, vmem, vmem],
        out_specs=(vmem,) * 3,
        compiler_params=pltpu.CompilerParams(vmem_limit_bytes=16 * MIB),
        cost_estimate=chunk_cost,
        name="attend_own",
    )(block_plan, doc_lengths, queries, key_vectors, value_vectors)
    for s in shifts[:-1]:
        state = pl.pallas_call(
            functools.partial(chunk_kernel, dims, s),
            out_shape=state_shapes,
            in_specs=[smem, smem] + [vmem] * 6,
            out_specs=(vmem,) * 3,
            compiler_params=pltpu.CompilerParams(vmem_limit_bytes=16 * MIB),
            cost_estimate=chunk_cost,
        )(block_plan, doc_lengths, queries, keys[s], values[s], *state)

    fulls = []
    for members in groups:
        mine = jnp.stack([w_z[s] for s in members])
        parts = []
        for mask in masks:
            part = mine
            if mask:
                part = from_dp(mine, mask)
            parts += [part, from_dp(part, 1)]
        fulls.append(
            pl.pallas_call(
                functools.partial(assemble_kernel, masks),
                out_shape=jax.ShapeDtypeStruct((len(members), depth, cols), jnp.bfloat16),
                in_specs=[vmem] * len(parts),
                out_specs=vmem,
                compiler_params=pltpu.CompilerParams(vmem_limit_bytes=16 * MIB),
                cost_estimate=pl.CostEstimate(flops=0, bytes_accessed=2 * MIB, transcendentals=0),
            )(*parts)
        )

    tile = min(cols, 512)
    last = shifts[-1]
    return pl.pallas_call(
        functools.partial(final_kernel, dims, last, groups, tile),
        out_shape=jax.ShapeDtypeStruct((rows, out_cols), jnp.bfloat16),
        in_specs=[smem, smem] + [vmem] * (7 + len(fulls)),
        out_specs=anyspace,
        scratch_shapes=[
            pltpu.VMEM((rows, width), jnp.bfloat16),
            pltpu.VMEM((ctx, rows, cols), jnp.bfloat16),
            pltpu.VMEM((2 * heads, half), jnp.float32),
            pltpu.VMEM((2 * heads, half), jnp.float32),
            pltpu.VMEM((2 * heads * hd, half), jnp.float32),
            pltpu.SemaphoreType.DMA((ctx, cols // tile)),
        ],
        compiler_params=pltpu.CompilerParams(vmem_limit_bytes=28 * MIB),
        cost_estimate=pl.CostEstimate(
            flops=2 * rows * depth * out_cols, bytes_accessed=8 * MIB, transcendentals=0
        ),
        name="project",
    )(block_plan, doc_lengths, queries, keys[last], values[last], *state, out_weight, *fulls)


def groups_of(ctx):
    shifts = list(range(1, ctx))
    return [shifts[:-1], shifts[-1:]] if ctx > 2 else [shifts]


def solution(mesh):
    placed = (
        P(("dp", "ctx"), None),
        P(("dp", "ctx"), None),
        P(("dp", "ctx"), None),
        P("dp"),
        P("dp"),
        P(None, "ctx"),
    )
    body = functools.partial(shards, mesh.shape["dp"], mesh.shape["ctx"])
    return jax.shard_map(body, mesh=mesh, in_specs=placed, out_specs=P(("dp", "ctx"), None), check_vma=False)
```

```python
import functools
import math

import jax
import jax.numpy as jnp
from jax import lax
from jax.experimental import pallas as pl
from jax.experimental.pallas import tpu as pltpu
from jax.sharding import PartitionSpec as P


NEG = -1e30
MIB = 1 << 20


def doc_start(lengths_ref, position):
    end = jnp.int32(0)
    start = jnp.zeros_like(position)
    for i in range(lengths_ref.shape[0]):
        end = end + lengths_ref[i]
        start = jnp.maximum(start, jnp.where(position >= end, end, 0))
    return start


def scalar_start(lengths_ref, position):
    end = jnp.int32(0)
    start = jnp.int32(0)
    for i in range(lengths_ref.shape[0]):
        end = end + lengths_ref[i]
        start = jnp.maximum(start, jnp.where(position >= end, end, 0))
    return start


def attend_pair(dims, first, diagonal, q_blk, k_blk, start, key_base, q_ref, kv_ref, m_ref, l_ref, acc_ref):
    half, hd, heads, scale = dims
    wide = heads * half
    key = kv_ref[0, k_blk * half:(k_blk + 1) * half, :]
    value_t = kv_ref[1, k_blk * half:(k_blk + 1) * half, :].astype(jnp.float32).T.astype(jnp.bfloat16)
    key_ids = lax.broadcasted_iota(jnp.int32, (half, half), 0)
    keep = key_ids >= start - key_base
    if diagonal:
        keep = keep & (key_ids <= lax.broadcasted_iota(jnp.int32, (half, half), 1))
    bias = jnp.where(keep, jnp.float32(0.0), jnp.float32(NEG))
    bias = jnp.concatenate([bias] * heads, axis=1)
    query = q_ref[q_blk * wide:(q_blk + 1) * wide, :]
    s = lax.dot_general(key, query, (((1,), (1,)), ((), ())), preferred_element_type=jnp.float32)
    t = s * scale + bias
    top = jnp.max(t, axis=0, keepdims=True)
    at = slice(q_blk, q_blk + 1)
    rows = slice(q_blk * hd, (q_blk + 1) * hd)
    if first:
        m_new = top
    else:
        m_old = m_ref[at, :]
        m_new = jnp.maximum(m_old, top)
    p = jnp.exp2(t - m_new)
    total = jnp.sum(p, axis=0, keepdims=True)
    part = jnp.dot(value_t, p.astype(jnp.bfloat16), preferred_element_type=jnp.float32)
    if first:
        l_ref[at, :] = total
        acc_ref[rows, :] = part
    else:
        alpha = jnp.exp2(m_old - m_new)
        l_ref[at, :] = l_ref[at, :] * alpha + total
        acc_ref[rows, :] = acc_ref[rows, :] * alpha + part
    m_ref[at, :] = m_new


def attend_chunk(dims, own, me, src, plan_ref, lengths_ref, *args):
    half = dims[0]
    order = [(0, 0), (1, 1), (0, 1), (1, 0)]
    lanes = lax.broadcasted_iota(jnp.int32, (1, half), 1)
    for q_blk, k_blk in order:
        q_base = plan_ref[me * 2 + q_blk] * half
        k_base = plan_ref[src * 2 + k_blk] * half
        if own and q_blk == k_blk:
            start = doc_start(lengths_ref, q_base + lanes)
            attend_pair(dims, True, True, q_blk, k_blk, start, k_base, *args)
        else:
            need = (k_base < q_base) & (scalar_start(lengths_ref, q_base) < k_base + half)

            @pl.when(need)
            def _(q_blk=q_blk, k_blk=k_blk, q_base=q_base, k_base=k_base):
                start = doc_start(lengths_ref, q_base + lanes)
                attend_pair(dims, False, False, q_blk, k_blk, start, k_base, *args)


def pack_kernel(k_ref, v_ref, w_ref, kv_ref, piece_ref, sem):
    rows = piece_ref.shape[0]
    base = pl.multiple_of(lax.axis_index("dp") * rows, rows)
    copies = [
        pltpu.make_async_copy(k_ref, kv_ref.at[0], sem.at[0]),
        pltpu.make_async_copy(v_ref, kv_ref.at[1], sem.at[1]),
        pltpu.make_async_copy(w_ref.at[pl.ds(base, rows), :], piece_ref, sem.at[2]),
    ]
    for copy in copies:
        copy.start()
    for copy in copies:
        copy.wait()


def own_kernel(dims, plan_hbm, lengths_hbm, q_hbm, kv_ref, q_ref, m_ref, l_ref, acc_ref, plan_ref, lengths_ref, sem):
    half, hd, heads, _ = dims
    me = lax.axis_index("ctx")
    copies = [
        pltpu.make_async_copy(plan_hbm, plan_ref, sem.at[0]),
        pltpu.make_async_copy(lengths_hbm, lengths_ref, sem.at[1]),
    ]
    for q_blk in range(2):
        for h in range(heads):
            row = (q_blk * heads + h) * half
            copies.append(
                pltpu.make_async_copy(
                    q_hbm.at[pl.ds(q_blk * half, half), pl.ds(h * hd, hd)],
                    q_ref.at[pl.ds(row, half), :],
                    sem.at[2 + q_blk * heads + h],
                )
            )
    for copy in copies:
        copy.start()
    for copy in copies:
        copy.wait()
    attend_chunk(dims, True, me, me, plan_ref, lengths_ref, q_ref, kv_ref, m_ref, l_ref, acc_ref)


def chunk_kernel(
    dims, shift, plan_hbm, lengths_hbm, q_ref, kv_ref, m_in, l_in, acc_in, m_ref, l_ref, acc_ref, plan_ref, lengths_ref, sem
):
    me = lax.axis_index("ctx")
    copies = [
        pltpu.make_async_copy(plan_hbm, plan_ref, sem.at[0]),
        pltpu.make_async_copy(lengths_hbm, lengths_ref, sem.at[1]),
    ]
    for copy in copies:
        copy.start()
    for source, target in ((m_in, m_ref), (l_in, l_ref), (acc_in, acc_ref)):
        target[...] = source[...]
    for copy in copies:
        copy.wait()
    attend_chunk(dims, False, me, me ^ shift, plan_ref, lengths_ref, q_ref, kv_ref, m_ref, l_ref, acc_ref)


def assemble_kernel(masks, *refs):
    part_refs, full_ref = refs[:-1], refs[-1]
    dp = lax.axis_index("dp")
    rows = part_refs[0].shape[1]
    for j, mask in enumerate(masks):
        for core in range(2):
            row = pl.multiple_of((dp ^ (mask ^ core)) * rows, rows)
            for i in range(full_ref.shape[0]):
                full_ref[i, pl.ds(row, rows), :] = part_refs[2 * j + core][i]


def final_kernel(dims, groups, tile, l_ref, acc_ref, w_ref, *refs):
    half, hd, heads, _ = dims
    full_refs = refs[:len(groups)]
    out_ref, att, stage, o_sem = refs[len(groups):]
    me = lax.axis_index("ctx")
    cols = w_ref.shape[1]
    for q_blk in range(2):
        o = acc_ref[q_blk * hd:(q_blk + 1) * hd, :] / l_ref[q_blk:q_blk + 1, :]
        for h in range(heads):
            block = o[:, h * half:(h + 1) * half].T
            att[q_blk * half:(q_blk + 1) * half, h * hd:(h + 1) * hd] = block.astype(jnp.bfloat16)
    weights = [(0, w_ref)]
    for full_ref, shifts in zip(full_refs, groups):
        weights += [(s, full_ref.at[i]) for i, s in enumerate(shifts)]
    stores = []
    for slot, (s, weight) in enumerate(weights):
        base = (me ^ s) * cols
        for t in range(0, cols, tile):
            y = jnp.dot(att[...], weight[:, t:t + tile], preferred_element_type=jnp.float32)
            stage[slot, :, t:t + tile] = y.astype(jnp.bfloat16)
            store = pltpu.make_async_copy(
                stage.at[slot, :, pl.ds(t, tile)],
                out_ref.at[:, pl.ds(pl.multiple_of(base + t, tile), tile)],
                o_sem.at[slot, t // tile],
            )
            store.start()
            stores.append(store)
    for store in stores:
        store.wait()


def shards(dp_size, ctx, *args):
    return run(dp_size, ctx, *args)


def run(dp_size, ctx, queries, key_vectors, value_vectors, block_plan, doc_lengths, out_weight):
    rows, width = queries.shape
    hd = key_vectors.shape[1]
    heads = width // hd
    half = rows // 2
    depth, cols = out_weight.shape
    out_cols = cols * ctx
    piece_rows = depth // dp_size
    dims = (half, hd, heads, math.log2(math.e) / math.sqrt(hd))
    shifts = list(range(1, ctx))
    masks = list(range(0, dp_size, 2))
    groups = groups_of(ctx)
    vmem = pl.BlockSpec(memory_space=pltpu.VMEM)
    hbm = pl.BlockSpec(memory_space=pltpu.HBM)

    def in_hbm(x):
        return pltpu.with_memory_space_constraint(x, pltpu.HBM)

    def params(mib):
        return pltpu.CompilerParams(vmem_limit_bytes=mib * MIB)

    def from_ctx(x, s):
        return lax.ppermute(x, "ctx", [(i ^ s, i) for i in range(ctx)])

    def from_dp(x, mask):
        return lax.ppermute(x, "dp", [(i ^ mask, i) for i in range(dp_size)])

    kv_own, piece = pl.pallas_call(
        pack_kernel,
        out_shape=(
            jax.ShapeDtypeStruct((2, rows, hd), jnp.bfloat16),
            jax.ShapeDtypeStruct((piece_rows, cols), jnp.bfloat16),
        ),
        in_specs=[hbm] * 3,
        out_specs=(vmem, vmem),
        scratch_shapes=[pltpu.SemaphoreType.DMA((3,))],
        compiler_params=params(4),
        name="pack",
    )(in_hbm(key_vectors), in_hbm(value_vectors), in_hbm(out_weight))
    kv, w_z = {}, {}
    for s in shifts:
        kv[s] = from_ctx(kv_own, s)
    for s in shifts:
        w_z[s] = from_ctx(piece, s)

    state_shapes = (
        jax.ShapeDtypeStruct((2, heads * half), jnp.float32),
        jax.ShapeDtypeStruct((2, heads * half), jnp.float32),
        jax.ShapeDtypeStruct((2 * hd, heads * half), jnp.float32),
    )
    chunk_cost = pl.CostEstimate(
        flops=4 * heads * rows * rows * hd, bytes_accessed=3 * MIB, transcendentals=heads * rows * rows
    )
    stacked, *state = pl.pallas_call(
        functools.partial(own_kernel, dims),
        out_shape=(jax.ShapeDtypeStruct((rows * heads, hd), jnp.bfloat16),) + state_shapes,
        in_specs=[hbm, hbm, hbm, vmem],
        out_specs=(vmem,) * 4,
        scratch_shapes=[
            pltpu.SMEM(block_plan.shape, jnp.int32),
            pltpu.SMEM(doc_lengths.shape, jnp.int32),
            pltpu.SemaphoreType.DMA((2 + 2 * heads,)),
        ],
        compiler_params=params(16),
        cost_estimate=chunk_cost,
        name="attend_own",
    )(in_hbm(block_plan), in_hbm(doc_lengths), in_hbm(queries), kv_own)
    for s in shifts:
        state = pl.pallas_call(
            functools.partial(chunk_kernel, dims, s),
            out_shape=state_shapes,
            in_specs=[hbm, hbm] + [vmem] * 5,
            out_specs=(vmem,) * 3,
            scratch_shapes=[
                pltpu.SMEM(block_plan.shape, jnp.int32),
                pltpu.SMEM(doc_lengths.shape, jnp.int32),
                pltpu.SemaphoreType.DMA((2,)),
            ],
            compiler_params=params(16),
            cost_estimate=chunk_cost,
        )(in_hbm(block_plan), in_hbm(doc_lengths), stacked, kv[s], *state)

    fulls = []
    for members in groups:
        mine = jnp.stack([w_z[s] for s in members])
        parts = []
        for mask in masks:
            part = mine
            if mask:
                part = from_dp(mine, mask)
            parts += [part, from_dp(part, 1)]
        fulls.append(
            pl.pallas_call(
                functools.partial(assemble_kernel, masks),
                out_shape=jax.ShapeDtypeStruct((len(members), depth, cols), jnp.bfloat16),
                in_specs=[vmem] * len(parts),
                out_specs=vmem,
                compiler_params=params(16),
                cost_estimate=pl.CostEstimate(flops=0, bytes_accessed=2 * MIB, transcendentals=0),
            )(*parts)
        )

    tile = min(cols, 512)
    return pl.pallas_call(
        functools.partial(final_kernel, dims, groups, tile),
        out_shape=jax.ShapeDtypeStruct((rows, out_cols), jnp.bfloat16),
        in_specs=[vmem] * (3 + len(fulls)),
        out_specs=hbm,
        scratch_shapes=[
            pltpu.VMEM((rows, width), jnp.bfloat16),
            pltpu.VMEM((ctx, rows, cols), jnp.bfloat16),
            pltpu.SemaphoreType.DMA((ctx, cols // tile)),
        ],
        compiler_params=params(24),
        cost_estimate=pl.CostEstimate(
            flops=2 * rows * depth * out_cols, bytes_accessed=8 * MIB, transcendentals=0
        ),
        name="project",
    )(state[1], state[2], out_weight, *fulls)


def groups_of(ctx):
    return [list(range(1, ctx))]


def solution(mesh):
    placed = (
        P(("dp", "ctx"), None),
        P(("dp", "ctx"), None),
        P(("dp", "ctx"), None),
        P("dp"),
        P("dp"),
        P(None, "ctx"),
    )
    body = functools.partial(shards, mesh.shape["dp"], mesh.shape["ctx"])
    return jax.shard_map(body, mesh=mesh, in_specs=placed, out_specs=P(("dp", "ctx"), None), check_vma=False)
```
